32 devices in a mesh: seq: 8 (over z, y), tensor: 4 (over x, core).
Axes of the slice: x: 2, y: 2, z: 4, core: 2. Of those that a mesh axis runs over, the one named last changes fastest.
Arguments:
- residual: bfloat16 [4608, 6144], P('seq', 'tensor'), may hold values from -4 to 4
- queries: bfloat16 [4608, 4096], P(('seq', 'tensor')), may hold values from -6 to 6
- key_rows: bfloat16 [4608, 4096], P(('seq', 'tensor')), may hold values from -6 to 6
- value_rows: bfloat16 [4608, 4096], P(('seq', 'tensor')), may hold values from -6 to 6
- w_out: bfloat16 [4096, 6144], P(None, 'tensor'), may hold values from -0.09375 to 0.09375
- out_gate: float32 [6144], P('tensor'), may hold values from 0.5 to 1.5
- extents: int32 [32, 3], replicated, may hold values from 0 to 1, as said below
Outputs:
- updated: bfloat16 [4608, 6144], P('seq', 'tensor')
The draws below stay inside these ranges and needn't reach their ends.
Inputs may be any that keep to these rules, and one draw needn't show every extreme that they name: `extents`: reaches in tile-frames are at most 1, in tile-rows at most 1, in tile-columns at most 1; each of these bounds is taken by some head, and some head has reach 0 in tile-rows.
All inputs are finite; a program needn't handle non-finite values.
Results may differ from the reference program's by a relative error of at most 0.0048.
Values may be sent and summed in bfloat16 or wider, within the bound.
A program may use at most 192 MiB of HBM per device.

```python
import math
import jax
import jax.numpy as jnp
from jax import lax

D = 6144
HEAD_DIM = 128
HEADS = 32
TILE = 32
FT = 3
HT_DEV = 2
WT = 3
INNER = 4096
S_DEV = 576
TOKENS = 4608
N_SEQ = 8


def draw_pair(key):
    base_key = jax.random.fold_in(key, 71)
    key_q, key_k = jax.random.split(base_key, 2)
    query_part = jnp.clip(1.4 * jax.random.normal(key_q, (TOKENS, INNER), jnp.float32), -6.0, 6.0)
    key_part = jnp.clip(1.4 * jax.random.normal(key_k, (TOKENS, INNER), jnp.float32), -6.0, 6.0)
    return (query_part, key_part)


def draw_queries(key, part):
    return draw_pair(key)[0].astype(jnp.bfloat16)


def draw_key_rows(key, part):
    return draw_pair(key)[1].astype(jnp.bfloat16)


def draw_extents(key, part):
    base_key = jax.random.fold_in(key, 29)
    keys_all = jax.random.split(base_key, 6)
    head_ids = jnp.arange(HEADS, dtype=jnp.int32)
    frame_most = min(FT - 1, 1)
    col_most = min(WT - 1, 1)
    frames_reach = jax.random.randint(keys_all[0], (HEADS,), 0, frame_most + 1)
    rows_reach = jax.random.randint(keys_all[1], (HEADS,), 0, 2)
    cols_reach = jax.random.randint(keys_all[2], (HEADS,), 0, col_most + 1)
    pick_frame = jax.random.randint(keys_all[3], (), 0, HEADS)
    pick_row = jax.random.randint(keys_all[4], (), 0, HEADS)
    pick_col = jax.random.randint(keys_all[5], (), 0, HEADS)
    frames_reach = jnp.where(head_ids == pick_frame, frame_most, frames_reach)
    rows_reach = jnp.where(head_ids == (pick_row + 1) % HEADS, 0, rows_reach)
    rows_reach = jnp.where(head_ids == pick_row, 1, rows_reach)
    cols_reach = jnp.where(head_ids == pick_col, col_most, cols_reach)
    return jnp.stack([frames_reach, rows_reach, cols_reach], axis=1).astype(jnp.int32)


def block_levels(key, dims, cuts, least, largest):
    level, own = 1.0, jax.random.fold_in(key, 6)
    for axis_at, blocks in cuts:
        steps = jnp.exp(jax.random.uniform(jax.random.fold_in(own, axis_at), (blocks,), jnp.float32, least / len(cuts), largest / len(cuts)))
        level = level * jnp.repeat(steps, dims[axis_at] // blocks).reshape([-1 if axis == axis_at else 1 for axis in range(len(dims))])
    return level


def bell_draw(rng, extent, spread, reach, cuts=(), held_as=jnp.bfloat16):
    drawn = spread * jax.random.normal(rng, extent, jnp.float32)
    if cuts:
        drawn = drawn * block_levels(rng, extent, cuts, -0.22, 0.18)
    return jnp.clip(drawn, -reach, reach).astype(held_as)


def setup_inputs(seed: int = 0) -> dict:
    key_of = jax.random.split(jax.random.key(seed), 8)
    return {
        "residual": bell_draw(key_of[0], (TOKENS, D), 0.5, 4.0, ((0, 8), (1, 4))),
        "queries": draw_queries(jax.random.fold_in(key_of[7], 71), 0),
        "key_rows": draw_key_rows(jax.random.fold_in(key_of[7], 71), 0),
        "value_rows": bell_draw(key_of[3], (TOKENS, INNER), 1.0, 6.0, ((0, 32),)),
        "w_out": bell_draw(key_of[4], (INNER, D), INNER ** -0.5, 0.09375, ((1, 4),)),
        "out_gate": jnp.clip(0.5 + 1.0 * jax.random.uniform(key_of[5], (D,), jnp.float32) ** block_levels(key_of[5], (D,), ((0, 4),), -0.2, 0.2), 0.5, 1.5),
        "extents": draw_extents(jax.random.fold_in(key_of[7], 71), 0),
    }


def tile_coords(row_count, tile_rows, first_row):
    position = jnp.arange(row_count, dtype=jnp.int32)
    frame_id = position // (tile_rows * WT * TILE)
    row_id = first_row + position // (WT * TILE) % tile_rows
    col_id = position // TILE % WT
    return (frame_id, row_id, col_id)

def allowed_keys(query_place, key_place, head_reach, seq_block, seq_count):
    frame_gap = jnp.abs(query_place[0][:, None] - key_place[0][None, :])
    row_gap = jnp.abs(query_place[1][:, None] - key_place[1][None, :])
    col_gap = jnp.abs(query_place[2][:, None] - key_place[2][None, :])
    global_row = key_place[1] + seq_block * HT_DEV
    inside = (global_row >= 0) & (global_row < seq_count * HT_DEV)
    return (frame_gap[None] <= head_reach[:, 0, None, None]) & (row_gap[None] <= head_reach[:, 1, None, None]) & (col_gap[None] <= head_reach[:, 2, None, None]) & inside[None, None, :]

def reference(residual, queries, key_rows, value_rows, w_out, out_gate, extents):
    zero_rows = jnp.zeros((S_DEV, INNER), jnp.bfloat16)
    keys_padded = jnp.concatenate([zero_rows, key_rows, zero_rows], 0)
    values_padded = jnp.concatenate([zero_rows, value_rows, zero_rows], 0)
    query_place = tile_coords(S_DEV, HT_DEV, 0)
    three_parts = [tile_coords(S_DEV, HT_DEV, first) for first in (-HT_DEV, 0, HT_DEV)]
    key_place = tuple((jnp.concatenate([part[axis_id] for part in three_parts]) for axis_id in range(3)))

    def one_head(head_id):
        query_cols = lax.dynamic_slice_in_dim(queries, head_id * HEAD_DIM, HEAD_DIM, 1)
        key_cols = lax.dynamic_slice_in_dim(keys_padded, head_id * HEAD_DIM, HEAD_DIM, 1)
        value_cols = lax.dynamic_slice_in_dim(values_padded, head_id * HEAD_DIM, HEAD_DIM, 1)
        head_reach = lax.dynamic_slice_in_dim(extents, head_id, 1, 0)

        def one_block(seq_block):
            q_tile = lax.dynamic_slice_in_dim(query_cols, seq_block * S_DEV, S_DEV, 0)
            k_tile = lax.dynamic_slice_in_dim(key_cols, seq_block * S_DEV, 3 * S_DEV, 0)
            v_tile = lax.dynamic_slice_in_dim(value_cols, seq_block * S_DEV, 3 * S_DEV, 0)
            scores = jnp.dot(q_tile, k_tile.T, preferred_element_type=jnp.float32) / math.sqrt(HEAD_DIM)
            allowed = allowed_keys(query_place, key_place, head_reach, seq_block, N_SEQ)[0]
            scores = jnp.where(allowed, scores, -1e+30)
            row_max = lax.optimization_barrier(jnp.max(scores, axis=-1, keepdims=True))
            exp_scores = jnp.exp(scores - row_max)
            row_sum = lax.optimization_barrier(jnp.sum(exp_scores, axis=-1, keepdims=True))
            weights = (exp_scores / row_sum).astype(jnp.bfloat16)
            return jnp.dot(weights, v_tile, preferred_element_type=jnp.float32).astype(jnp.bfloat16)
        blocks = lax.map(one_block, jnp.arange(N_SEQ, dtype=jnp.int32))
        return blocks.reshape(TOKENS, HEAD_DIM)
    per_head = lax.map(one_head, jnp.arange(HEADS, dtype=jnp.int32))
    attended = per_head.transpose(1, 0, 2).reshape(TOKENS, INNER)
    projected = jnp.dot(attended, w_out, preferred_element_type=jnp.float32)
    return (residual.astype(jnp.float32) + out_gate * projected).astype(jnp.bfloat16)
```

```python
import functools
import math

import jax
import jax.numpy as jnp
import numpy as np
from jax import lax
from jax.experimental import pallas as pl
from jax.experimental.pallas import tpu as pltpu
from jax.sharding import PartitionSpec as P

HEAD_DIM = 128
TILE = 32
HT_DEV = 2
WT = 3
CHUNK_HEADS = 2
FAR = -1e30
MESH = pl.DeviceIdType.MESH


def passed_along(value, axis, by):
    length = lax.axis_size(axis)
    pairs = [(i, i + by) for i in range(length) if 0 <= i + by < length]
    return lax.ppermute(value, axis, pairs)


def tile_coords(row_count, tile_rows, first_row):
    position = jnp.arange(row_count, dtype=jnp.int32)
    frame_id = position // (tile_rows * WT * TILE)
    row_id = first_row + position // (WT * TILE) % tile_rows
    col_id = position // TILE % WT
    return (frame_id, row_id, col_id)


def allowed_keys(query_place, key_place, head_reach, seq_block, seq_count):
    frame_gap = jnp.abs(query_place[0][:, None] - key_place[0][None, :])
    row_gap = jnp.abs(query_place[1][:, None] - key_place[1][None, :])
    col_gap = jnp.abs(query_place[2][:, None] - key_place[2][None, :])
    global_row = key_place[1] + seq_block * HT_DEV
    inside = (global_row >= 0) & (global_row < seq_count * HT_DEV)
    return (
        (frame_gap[None] <= head_reach[:, 0, None, None])
        & (row_gap[None] <= head_reach[:, 1, None, None])
        & (col_gap[None] <= head_reach[:, 2, None, None])
        & inside[None, None, :]
    )


def plain_shards(residual, queries, key_rows, value_rows, w_out, out_gate, extents):
    head_q, head_k, head_v = (
        lax.all_to_all(queries, "tensor", split_axis=1, concat_axis=0, tiled=True),
        lax.all_to_all(key_rows, "tensor", split_axis=1, concat_axis=0, tiled=True),
        lax.all_to_all(value_rows, "tensor", split_axis=1, concat_axis=0, tiled=True),
    )
    tokens, inner_dev = head_q.shape
    heads_here = inner_dev // HEAD_DIM
    seq_block = lax.axis_index("seq")
    seq_count = lax.axis_size("seq")
    head_reach = lax.dynamic_slice_in_dim(
        extents, lax.axis_index("tensor") * heads_here, heads_here, 0
    )
    query_tiles = head_q.reshape(tokens, heads_here, HEAD_DIM)
    query_place = tile_coords(tokens, HT_DEV, 0)
    stacked = jnp.stack([head_k, head_v])

    def part_scores(pair_rows, key_place):
        key_tiles = pair_rows[0].reshape(-1, heads_here, HEAD_DIM)
        scores = jnp.einsum(
            "qhd,khd->hqk", query_tiles, key_tiles, preferred_element_type=jnp.float32
        ) / math.sqrt(HEAD_DIM)
        allowed = allowed_keys(query_place, key_place, head_reach, seq_block, seq_count)
        return jnp.where(allowed, scores, FAR)

    by_row = stacked.reshape(2, -1, HT_DEV, WT * TILE, inner_dev)
    halves = tokens // HT_DEV
    last_row = by_row[:, :, HT_DEV - 1].reshape(2, halves, inner_dev)
    first_row = by_row[:, :, 0].reshape(2, halves, inner_dev)
    parts = [
        (stacked, query_place),
        (passed_along(last_row, "seq", 1), tile_coords(halves, 1, -1)),
        (passed_along(first_row, "seq", -1), tile_coords(halves, 1, HT_DEV)),
    ]
    scores = jnp.concatenate([part_scores(*part) for part in parts], axis=-1)
    value_all = jnp.concatenate([pair_rows[1] for pair_rows, _ in parts], axis=0)
    row_max = jnp.max(scores, axis=-1, keepdims=True)
    exp_scores = jnp.exp(scores - row_max)
    row_sum = jnp.sum(exp_scores, axis=-1, keepdims=True)
    weights = (exp_scores / row_sum).astype(jnp.bfloat16)
    attended = jnp.einsum(
        "hqk,khd->qhd",
        weights,
        value_all.reshape(-1, heads_here, HEAD_DIM),
        preferred_element_type=jnp.float32,
    )
    head_out = attended.reshape(tokens, inner_dev).astype(jnp.bfloat16)
    projected = jnp.dot(
        lax.all_gather(head_out, "tensor", axis=1, tiled=True),
        w_out,
        preferred_element_type=jnp.float32,
    )
    return (residual.astype(jnp.float32) + out_gate * projected).astype(jnp.bfloat16)


def mask_features(frames):
    span = WT * TILE
    q_feat = np.zeros((2, frames * span, HEAD_DIM), np.float32)
    k_feat = np.zeros((2, frames * 3 * span, HEAD_DIM), np.float32)
    q_at = np.arange(frames * span)
    q_frame, q_col = q_at // span, q_at // TILE % WT
    k_at = np.arange(frames * 3 * span)
    k_frame, k_col = k_at // (3 * span), k_at // TILE % WT
    k_row = k_at // span % 3 - 1
    for r in range(2):
        for j in range(3):
            q_feat[r, :, j] = q_feat[r, :, 8 + j] = q_frame == j
            q_feat[r, :, 3 + j] = q_feat[r, :, 11 + j] = q_col == j
            k_feat[r, :, j] = FAR * (abs(k_frame - j) >= 2)
            k_feat[r, :, 8 + j] = FAR * (abs(k_frame - j) == 1)
            k_feat[r, :, 3 + j] = FAR * (abs(k_col - j) >= 2)
            k_feat[r, :, 11 + j] = FAR * (abs(k_col - j) == 1)
        q_feat[r, :, 14:17] = 1.0
        k_feat[r, :, 14] = FAR * (k_row != 0)
    k_feat[0, :, 15] = FAR * (k_row == -1)
    k_feat[1, :, 16] = FAR * (k_row == 1)
    return jnp.asarray(q_feat, jnp.bfloat16), jnp.asarray(k_feat, jnp.bfloat16)


def kernel(
    n_t, n_s, frames, q_hbm, k_hbm, v_hbm, w_hbm, res_hbm, gate_ref, coef_ref, qf_ref, kf_ref,
    out_ref, own, halo, gat, wbuf, res, acc,
    a_send, a_recv, a_loc, h_send, h_recv, g_send, g_recv, w_sem, r_sem,
):
    rows = q_hbm.shape[0]
    inner_dev = q_hbm.shape[1] // n_t
    width = CHUNK_HEADS * HEAD_DIM
    chunks = inner_dev // width
    span = WT * TILE
    me, sb = lax.axis_index("tensor"), lax.axis_index("seq")
    mate = me // 2 * 2 + 1 - lax.rem(me, 2)
    across = lax.rem(me + n_t // 2, n_t)
    srcs = (k_hbm, v_hbm, q_hbm)
    has_up, has_down = sb < n_s - 1, sb > 0

    barrier = pltpu.get_barrier_semaphore()
    for d in range(1, n_t):
        pl.semaphore_signal(
            barrier, inc=1, device_id={"tensor": lax.rem(me + d, n_t)}, device_id_type=MESH
        )

    @pl.when(has_up)
    def _():
        pl.semaphore_signal(barrier, inc=1, device_id={"seq": sb + 1}, device_id_type=MESH)

    @pl.when(has_down)
    def _():
        pl.semaphore_signal(barrier, inc=1, device_id={"seq": sb - 1}, device_id_type=MESH)

    inner_block = has_up & has_down

    @pl.when(inner_block)
    def _():
        pl.semaphore_wait(barrier, n_t + 1)

    @pl.when(jnp.logical_not(inner_block))
    def _():
        pl.semaphore_wait(barrier, n_t)

    def columns(owner, c):
        return pl.ds(pl.multiple_of(owner * inner_dev + c * width, width), width)

    def slot(owner):
        return pl.ds(pl.multiple_of(owner * rows, 16), rows)

    def sent(a, c, d, owner):
        peer = lax.rem(me + d, n_t)
        return pltpu.make_async_remote_copy(
            src_ref=srcs[a].at[:, columns(peer, c)],
            dst_ref=own.at[a, c, slot(owner), :],
            send_sem=a_send.at[a, c, d - 1],
            recv_sem=a_recv.at[a, c, d - 1],
            device_id={"tensor": peer},
            device_id_type=MESH,
        )

    def kept(a, c):
        return pltpu.make_async_copy(
            srcs[a].at[:, columns(me, c)], own.at[a, c, slot(me), :], a_loc.at[a, c]
        )

    def arrived(a, c):
        for d in range(1, n_t):
            sent(a, c, d, lax.rem(me - d + n_t, n_t)).wait_recv()
        kept(a, c).wait()

    def edge(way, a, c, f):
        first = f * 2 * span + (span if way == 0 else 0)
        return pltpu.make_async_remote_copy(
            src_ref=own.at[a, c, pl.ds(first, span), :],
            dst_ref=halo.at[way, a, c, pl.ds(f * span, span), :],
            send_sem=h_send.at[way, a, c, f],
            recv_sem=h_recv.at[way, a, c, f],
            device_id={"seq": sb + 1 if way == 0 else sb - 1},
            device_id_type=MESH,
        )

    def shared(c, kind):
        piece = across if kind == 2 else me
        return pltpu.make_async_remote_copy(
            src_ref=gat.at[c, piece],
            dst_ref=gat.at[c, piece],
            send_sem=g_send.at[c, kind],
            recv_sem=g_recv.at[c, kind],
            device_id={"tensor": across if kind == 1 else mate},
            device_id_type=MESH,
        )

    def shared_in(c, kind):
        piece = (mate, across, lax.rem(mate + n_t // 2, n_t))[kind]
        return pltpu.make_async_remote_copy(
            src_ref=gat.at[c, piece],
            dst_ref=gat.at[c, piece],
            send_sem=g_send.at[c, kind],
            recv_sem=g_recv.at[c, kind],
            device_id={"tensor": across if kind == 1 else mate},
            device_id_type=MESH,
        )

    def weights_in(c, s):
        return pltpu.make_async_copy(
            w_hbm.at[pl.ds(pl.multiple_of(s * inner_dev + c * width, width), width), :],
            wbuf.at[c, pl.ds(s * width, width), :],
            w_sem.at[c, s],
        )

    @pl.loop(0, chunks)
    def _(c):
        for a in range(3):
            for d in (2, 1, 3):
                sent(a, c, d, me).start()
            kept(a, c).start()

    @pl.loop(0, chunks)
    def _(c):
        for s in range(n_t):
            weights_in(c, s).start()

    res_copy = pltpu.make_async_copy(res_hbm, res, r_sem)
    res_copy.start()
    acc[...] = jnp.zeros_like(acc)

    @pl.when(sb == 0)
    def _():
        halo[0] = jnp.zeros(halo.shape[1:], halo.dtype)

    @pl.when(sb == n_s - 1)
    def _():
        halo[1] = jnp.zeros(halo.shape[1:], halo.dtype)

    def halo_start(c):
        for a in range(2):
            arrived(a, c)

            @pl.when(has_up)
            def _():
                for f in range(frames):
                    edge(0, a, c, f).start()

            @pl.when(has_down)
            def _():
                for f in range(frames):
                    edge(1, a, c, f).start()

    def gathered(a, c, r, lanes):
        parts = []
        for f in range(frames):
            near = own[a, c, f * 2 * span : (f + 1) * 2 * span, lanes]
            far = halo[r, a, c, f * span : (f + 1) * span, lanes]
            parts += [far, near] if r == 0 else [near, far]
        return jnp.concatenate(parts, axis=0)

    def attend(c):
        arrived(2, c)
        for a in range(2):

            @pl.when(has_down)
            def _():
                for f in range(frames):
                    edge(0, a, c, f).wait_recv()

            @pl.when(has_up)
            def _():
                for f in range(frames):
                    edge(1, a, c, f).wait_recv()

        ones = jnp.ones((frames * 3 * span, HEAD_DIM), jnp.bfloat16)
        for h in range(CHUNK_HEADS):
            lanes = slice(h * HEAD_DIM, (h + 1) * HEAD_DIM)
            coef = coef_ref[c * CHUNK_HEADS + h]
            for r in range(2):
                q_part = jnp.concatenate(
                    [own[2, c, (2 * f + r) * span : (2 * f + r + 1) * span, lanes]
                     for f in range(frames)], axis=0)
                q_feat = (qf_ref[r].astype(jnp.float32) * coef).astype(jnp.bfloat16)
                scores = lax.dot_general(
                    jnp.concatenate([q_part, q_feat], axis=1),
                    jnp.concatenate([gathered(0, c, r, lanes), kf_ref[r]], axis=1),
                    (((1,), (1,)), ((), ())),
                    preferred_element_type=jnp.float32,
                )
                top = jnp.max(scores, axis=-1, keepdims=True)
                weights = jnp.exp2(
                    (scores - top) * (math.log2(math.e) / math.sqrt(HEAD_DIM))
                ).astype(jnp.bfloat16)
                both = jnp.dot(
                    weights,
                    jnp.concatenate([gathered(1, c, r, lanes), ones], axis=1),
                    preferred_element_type=jnp.float32,
                )
                done = (both[:, :HEAD_DIM] / both[:, HEAD_DIM:]).astype(jnp.bfloat16)
                for f in range(frames):
                    gat[c, me, (2 * f + r) * span : (2 * f + r + 1) * span, lanes] = done[
                        f * span : (f + 1) * span
                    ]
        shared(c, 1).start()
        shared(c, 0).start()

    n_tile = 512

    def project(c):
        shared_in(c, 0).wait_recv()
        shared_in(c, 2).wait_recv()
        for s in range(n_t):
            weights_in(c, s).wait()

        @pl.loop(0, acc.shape[1] // n_tile)
        def _(j):
            cols = pl.ds(pl.multiple_of(j * n_tile, n_tile), n_tile)
            lhs = jnp.concatenate([gat[c, s] for s in range(n_t)], axis=1)
            acc[:, cols] += jnp.dot(lhs, wbuf[c, :, cols], preferred_element_type=jnp.float32)

    halo_start(0)

    @pl.loop(0, chunks + 2)
    def _(s):
        @pl.when(s + 1 < chunks)
        def _():
            halo_start(s + 1)

        @pl.when(s >= 2)
        def _():
            project(s - 2)

        @pl.when((s >= 1) & (s <= chunks))
        def _():
            shared_in(s - 1, 1).wait_recv()
            shared(s - 1, 2).start()

        @pl.when(s < chunks)
        def _():
            attend(s)

    res_copy.wait()
    out_ref[...] = (res[...].astype(jnp.float32) + gate_ref[...] * acc[...]).astype(out_ref.dtype)

    @pl.loop(0, chunks)
    def _(c):
        for a in range(3):
            for d in range(1, n_t):
                sent(a, c, d, me).wait_send()
        for a in range(2):

            @pl.when(has_up)
            def _():
                for f in range(frames):
                    edge(0, a, c, f).wait_send()

            @pl.when(has_down)
            def _():
                for f in range(frames):
                    edge(1, a, c, f).wait_send()

        for kind in range(3):
            shared(c, kind).wait_send()


def shards(residual, queries, key_rows, value_rows, w_out, out_gate, extents):
    n_t, n_s = lax.axis_size("tensor"), lax.axis_size("seq")
    rows, inner = queries.shape
    tokens, out_cols = residual.shape
    inner_dev = inner // n_t
    width = CHUNK_HEADS * HEAD_DIM
    if n_t != 4 or n_s < 2 or rows % 16 or inner_dev % width or out_cols % 512:
        return plain_shards(
            residual, queries, key_rows, value_rows, w_out, out_gate, extents
        )
    heads_here = inner_dev // HEAD_DIM
    chunks = inner_dev // width
    frames = tokens // (HT_DEV * WT * TILE)
    half = tokens // HT_DEV
    reach = lax.dynamic_slice_in_dim(extents, lax.axis_index("tensor") * heads_here, heads_here, 0)
    stops = (reach < 1).astype(jnp.float32)
    sb = lax.axis_index("seq")
    at_edge = jnp.stack([sb == 0, sb == n_s - 1]).astype(jnp.float32)
    coef = jnp.concatenate(
        [
            jnp.ones((heads_here, 8), jnp.float32),
            jnp.repeat(stops[:, 0:1], 3, axis=1),
            jnp.repeat(stops[:, 2:3], 3, axis=1),
            stops[:, 1:2],
            jnp.broadcast_to(at_edge[None], (heads_here, 2)),
            jnp.zeros((heads_here, HEAD_DIM - 17), jnp.float32),
        ],
        axis=1,
    ).reshape(heads_here, 1, HEAD_DIM)
    q_feat, k_feat = mask_features(frames)
    hbm = pl.BlockSpec(memory_space=pl.ANY)
    vmem = pl.BlockSpec(memory_space=pltpu.VMEM)
    dma = pltpu.SemaphoreType.DMA
    bf16 = jnp.bfloat16
    return pl.pallas_call(
        functools.partial(kernel, n_t, n_s, frames),
        out_shape=jax.ShapeDtypeStruct((tokens, out_cols), bf16),
        in_specs=[hbm] * 5 + [vmem] * 4,
        out_specs=vmem,
        scratch_shapes=[
            pltpu.VMEM((3, chunks, tokens, width), bf16),
            pltpu.VMEM((2, 2, chunks, half, width), bf16),
            pltpu.VMEM((chunks, n_t, tokens, width), bf16),
            pltpu.VMEM((chunks, n_t * width, out_cols), bf16),
            pltpu.VMEM((tokens, out_cols), bf16),
            pltpu.VMEM((tokens, out_cols), jnp.float32),
            dma((3, chunks, n_t - 1)),
            dma((3, chunks, n_t - 1)),
            dma((3, chunks)),
            dma((2, 2, chunks, frames)),
            dma((2, 2, chunks, frames)),
            dma((chunks, 3)),
            dma((chunks, 3)),
            dma((chunks, n_t)),
            dma,
        ],
        compiler_params=pltpu.CompilerParams(
            collective_id=0, has_side_effects=True, vmem_limit_bytes=56 << 20
        ),
    )(
        queries, key_rows, value_rows, w_out, residual,
        out_gate.reshape(1, out_cols), coef, q_feat, k_feat,
    )


def solution(mesh):
    placed = (
        P("seq", "tensor"),
        P(("seq", "tensor"), None),
        P(("seq", "tensor"), None),
        P(("seq", "tensor"), None),
        P(None, "tensor"),
        P("tensor"),
        P(),
    )
    return jax.shard_map(
        shards, mesh=mesh, in_specs=placed, out_specs=P("seq", "tensor"), check_vma=False
    )
```

```python
import functools
import math

import jax
import jax.numpy as jnp
import numpy as np
from jax import lax
from jax.experimental import pallas as pl
from jax.experimental.pallas import tpu as pltpu
from jax.sharding import PartitionSpec as P

HEAD_DIM = 128
TILE = 32
HT_DEV = 2
WT = 3
CHUNK_HEADS = 2
OUT_TILE = 512
FAR = -1e30
MESH = pl.DeviceIdType.MESH


def passed_along(value, axis, by):
    length = lax.axis_size(axis)
    pairs = [(i, i + by) for i in range(length) if 0 <= i + by < length]
    return lax.ppermute(value, axis, pairs)


def tile_coords(row_count, tile_rows, first_row):
    position = jnp.arange(row_count, dtype=jnp.int32)
    frame_id = position // (tile_rows * WT * TILE)
    row_id = first_row + position // (WT * TILE) % tile_rows
    col_id = position // TILE % WT
    return (frame_id, row_id, col_id)


def allowed_keys(query_place, key_place, head_reach, seq_block, seq_count):
    frame_gap = jnp.abs(query_place[0][:, None] - key_place[0][None, :])
    row_gap = jnp.abs(query_place[1][:, None] - key_place[1][None, :])
    col_gap = jnp.abs(query_place[2][:, None] - key_place[2][None, :])
    global_row = key_place[1] + seq_block * HT_DEV
    inside = (global_row >= 0) & (global_row < seq_count * HT_DEV)
    return (
        (frame_gap[None] <= head_reach[:, 0, None, None])
        & (row_gap[None] <= head_reach[:, 1, None, None])
        & (col_gap[None] <= head_reach[:, 2, None, None])
        & inside[None, None, :]
    )


def plain_shards(residual, queries, key_rows, value_rows, w_out, out_gate, extents):
    head_q, head_k, head_v = (
        lax.all_to_all(queries, "tensor", split_axis=1, concat_axis=0, tiled=True),
        lax.all_to_all(key_rows, "tensor", split_axis=1, concat_axis=0, tiled=True),
        lax.all_to_all(value_rows, "tensor", split_axis=1, concat_axis=0, tiled=True),
    )
    tokens, inner_dev = head_q.shape
    heads_here = inner_dev // HEAD_DIM
    seq_block = lax.axis_index("seq")
    seq_count = lax.axis_size("seq")
    head_reach = lax.dynamic_slice_in_dim(
        extents, lax.axis_index("tensor") * heads_here, heads_here, 0
    )
    query_tiles = head_q.reshape(tokens, heads_here, HEAD_DIM)
    query_place = tile_coords(tokens, HT_DEV, 0)
    stacked = jnp.stack([head_k, head_v])

    def part_scores(pair_rows, key_place):
        key_tiles = pair_rows[0].reshape(-1, heads_here, HEAD_DIM)
        scores = jnp.einsum(
            "qhd,khd->hqk", query_tiles, key_tiles, preferred_element_type=jnp.float32
        ) / math.sqrt(HEAD_DIM)
        allowed = allowed_keys(query_place, key_place, head_reach, seq_block, seq_count)
        return jnp.where(allowed, scores, FAR)

    by_row = stacked.reshape(2, -1, HT_DEV, WT * TILE, inner_dev)
    halves = tokens // HT_DEV
    last_row = by_row[:, :, HT_DEV - 1].reshape(2, halves, inner_dev)
    first_row = by_row[:, :, 0].reshape(2, halves, inner_dev)
    parts = [
        (stacked, query_place),
        (passed_along(last_row, "seq", 1), tile_coords(halves, 1, -1)),
        (passed_along(first_row, "seq", -1), tile_coords(halves, 1, HT_DEV)),
    ]
    scores = jnp.concatenate([part_scores(*part) for part in parts], axis=-1)
    value_all = jnp.concatenate([pair_rows[1] for pair_rows, _ in parts], axis=0)
    row_max = jnp.max(scores, axis=-1, keepdims=True)
    exp_scores = jnp.exp(scores - row_max)
    row_sum = jnp.sum(exp_scores, axis=-1, keepdims=True)
    weights = (exp_scores / row_sum).astype(jnp.bfloat16)
    attended = jnp.einsum(
        "hqk,khd->qhd",
        weights,
        value_all.reshape(-1, heads_here, HEAD_DIM),
        preferred_element_type=jnp.float32,
    )
    head_out = attended.reshape(tokens, inner_dev).astype(jnp.bfloat16)
    projected = jnp.dot(
        lax.all_gather(head_out, "tensor", axis=1, tiled=True),
        w_out,
        preferred_element_type=jnp.float32,
    )
    return (residual.astype(jnp.float32) + out_gate * projected).astype(jnp.bfloat16)


def mask_features(frames):
    span = WT * TILE
    q_feat = np.zeros((2, frames * span, HEAD_DIM), np.float32)
    k_feat = np.zeros((2, frames * 3 * span, HEAD_DIM), np.float32)
    q_at = np.arange(frames * span)
    q_frame, q_col = q_at // span, q_at // TILE % WT
    k_at = np.arange(frames * 3 * span)
    k_frame, k_col = k_at // (3 * span), k_at // TILE % WT
    k_row = k_at // span % 3 - 1
    for r in range(2):
        for j in range(3):
            q_feat[r, :, j] = q_feat[r, :, 8 + j] = q_frame == j
            q_feat[r, :, 3 + j] = q_feat[r, :, 11 + j] = q_col == j
            k_feat[r, :, j] = FAR * (abs(k_frame - j) >= 2)
            k_feat[r, :, 8 + j] = FAR * (abs(k_frame - j) == 1)
            k_feat[r, :, 3 + j] = FAR * (abs(k_col - j) >= 2)
            k_feat[r, :, 11 + j] = FAR * (abs(k_col - j) == 1)
        q_feat[r, :, 14:17] = 1.0
        k_feat[r, :, 14] = FAR * (k_row != 0)
    k_feat[0, :, 15] = FAR * (k_row == -1)
    k_feat[1, :, 16] = FAR * (k_row == 1)
    return jnp.asarray(q_feat, jnp.bfloat16), jnp.asarray(k_feat, jnp.bfloat16)


def kernel(
    n_t, n_s, frames, q_hbm, k_hbm, v_hbm, w_hbm, res_hbm, qf_hbm, kf_hbm, gate_ref, ext_ref,
    out_hbm, own, halo, gat, wbuf, res, acc, out, qf, kf,
    a_send, a_recv, a_loc, h_send, h_recv, g_send, g_recv, w_sem, c_sem, o_sem,
):
    rows = q_hbm.shape[0]
    inner_dev = q_hbm.shape[1] // n_t
    width = CHUNK_HEADS * HEAD_DIM
    chunks = inner_dev // width
    span = WT * TILE
    me, sb = lax.axis_index("tensor"), lax.axis_index("seq")
    mate = me // 2 * 2 + 1 - lax.rem(me, 2)
    across = lax.rem(me + n_t // 2, n_t)
    srcs = (k_hbm, v_hbm, q_hbm)
    has_up, has_down = sb < n_s - 1, sb > 0

    barrier = pltpu.get_barrier_semaphore()
    for d in range(1, n_t):
        pl.semaphore_signal(
            barrier, inc=1, device_id={"tensor": lax.rem(me + d, n_t)}, device_id_type=MESH
        )

    @pl.when(has_up)
    def _():
        pl.semaphore_signal(barrier, inc=1, device_id={"seq": sb + 1}, device_id_type=MESH)

    @pl.when(has_down)
    def _():
        pl.semaphore_signal(barrier, inc=1, device_id={"seq": sb - 1}, device_id_type=MESH)

    inner_block = has_up & has_down

    @pl.when(inner_block)
    def _():
        pl.semaphore_wait(barrier, n_t + 1)

    @pl.when(jnp.logical_not(inner_block))
    def _():
        pl.semaphore_wait(barrier, n_t)

    def columns(owner, c):
        return pl.ds(pl.multiple_of(owner * inner_dev + c * width, width), width)

    def slot(owner):
        return pl.ds(pl.multiple_of(owner * rows, 16), rows)

    def sent(a, c, d, owner):
        peer = lax.rem(me + d, n_t)
        return pltpu.make_async_remote_copy(
            src_ref=srcs[a].at[:, columns(peer, c)],
            dst_ref=own.at[a, c, slot(owner), :],
            send_sem=a_send.at[a, c, d - 1],
            recv_sem=a_recv.at[a, c, d - 1],
            device_id={"tensor": peer},
            device_id_type=MESH,
        )

    def kept(a, c):
        return pltpu.make_async_copy(
            srcs[a].at[:, columns(me, c)], own.at[a, c, slot(me), :], a_loc.at[a, c]
        )

    def arrived(a, c):
        for d in range(1, n_t):
            sent(a, c, d, lax.rem(me - d + n_t, n_t)).wait_recv()
        kept(a, c).wait()

    def edge(way, a, c, f):
        first = f * 2 * span + (span if way == 0 else 0)
        return pltpu.make_async_remote_copy(
            src_ref=own.at[a, c, pl.ds(first, span), :],
            dst_ref=halo.at[way, a, c, pl.ds(f * span, span), :],
            send_sem=h_send.at[way, a, c, f],
            recv_sem=h_recv.at[way, a, c, f],
            device_id={"seq": sb + 1 if way == 0 else sb - 1},
            device_id_type=MESH,
        )

    def shared(c, h, kind):
        piece = across if kind == 2 else me
        return pltpu.make_async_remote_copy(
            src_ref=gat.at[c, h, piece],
            dst_ref=gat.at[c, h, piece],
            send_sem=g_send.at[c, h, kind],
            recv_sem=g_recv.at[c, h, kind],
            device_id={"tensor": across if kind == 1 else mate},
            device_id_type=MESH,
        )

    def shared_in(c, h, kind):
        piece = (mate, across, lax.rem(mate + n_t // 2, n_t))[kind]
        return pltpu.make_async_remote_copy(
            src_ref=gat.at[c, h, piece],
            dst_ref=gat.at[c, h, piece],
            send_sem=g_send.at[c, h, kind],
            recv_sem=g_recv.at[c, h, kind],
            device_id={"tensor": across if kind == 1 else mate},
            device_id_type=MESH,
        )

    def weights_in(c, s):
        return pltpu.make_async_copy(
            w_hbm.at[pl.ds(pl.multiple_of(s * inner_dev + c * width, width), width), :],
            wbuf.at[c, pl.ds(s * width, width), :],
            w_sem.at[c, s],
        )

    @pl.loop(0, chunks)
    def _(c):
        for a in range(3):
            for d in (2, 1, 3):
                sent(a, c, d, me).start()
            kept(a, c).start()

    @pl.loop(0, chunks)
    def _(c):
        for s in range(n_t):
            weights_in(c, s).start()

    consts = [
        pltpu.make_async_copy(src, dst, c_sem.at[i])
        for i, (src, dst) in enumerate(((qf_hbm, qf), (kf_hbm, kf), (res_hbm, res)))
    ]
    for copy in consts:
        copy.start()
    acc[...] = jnp.zeros_like(acc)

    @pl.when(sb == 0)
    def _():
        halo[0] = jnp.zeros(halo.shape[1:], halo.dtype)

    @pl.when(sb == n_s - 1)
    def _():
        halo[1] = jnp.zeros(halo.shape[1:], halo.dtype)

    def halo_start(c):
        for a in range(2):
            arrived(a, c)

            @pl.when(has_up)
            def _():
                for f in range(frames):
                    edge(0, a, c, f).start()

            @pl.when(has_down)
            def _():
                for f in range(frames):
                    edge(1, a, c, f).start()

    def gathered(a, c, r, lanes):
        parts = []
        for f in range(frames):
            near = own[a, c, f * 2 * span : (f + 1) * 2 * span, lanes]
            far = halo[r, a, c, f * span : (f + 1) * span, lanes]
            parts += [far, near] if r == 0 else [near, far]
        return jnp.concatenate(parts, axis=0)

    def switches(head):
        lane = lax.broadcasted_iota(jnp.int32, (1, HEAD_DIM), 1)
        at = me * (inner_dev // HEAD_DIM) + head
        coef = jnp.where(lane < 8, 1.0, 0.0)
        for d, first, last in ((0, 8, 11), (2, 11, 14), (1, 14, 15)):
            stop = (1 - ext_ref[d, at]).astype(jnp.float32)
            coef = jnp.where((lane >= first) & (lane < last), stop, coef)
        coef = jnp.where(lane == 15, jnp.where(sb == 0, 1.0, 0.0), coef)
        return jnp.where(lane == 16, jnp.where(sb == n_s - 1, 1.0, 0.0), coef)

    def attend(c):
        arrived(2, c)
        for a in range(2):

            @pl.when(has_down)
            def _():
                for f in range(frames):
                    edge(0, a, c, f).wait_recv()

            @pl.when(has_up)
            def _():
                for f in range(frames):
                    edge(1, a, c, f).wait_recv()

        ones = jnp.ones((frames * 3 * span, HEAD_DIM), jnp.bfloat16)
        for h in range(CHUNK_HEADS):
            lanes = slice(h * HEAD_DIM, (h + 1) * HEAD_DIM)
            coef = switches(c * CHUNK_HEADS + h)
            for r in range(2):
                q_part = jnp.concatenate(
                    [own[2, c, (2 * f + r) * span : (2 * f + r + 1) * span, lanes]
                     for f in range(frames)], axis=0)
                q_feat = (qf[r].astype(jnp.float32) * coef).astype(jnp.bfloat16)
                scores = lax.dot_general(
                    jnp.concatenate([q_part, q_feat], axis=1),
                    jnp.concatenate([gathered(0, c, r, lanes), kf[r]], axis=1),
                    (((1,), (1,)), ((), ())),
                    preferred_element_type=jnp.float32,
                )
                top = jnp.max(scores, axis=-1, keepdims=True)
                weights = jnp.exp2(
                    (scores - top) * (math.log2(math.e) / math.sqrt(HEAD_DIM))
                ).astype(jnp.bfloat16)
                both = jnp.dot(
                    weights,
                    jnp.concatenate([gathered(1, c, r, lanes), ones], axis=1),
                    preferred_element_type=jnp.float32,
                )
                done = (both[:, :HEAD_DIM] / both[:, HEAD_DIM:]).astype(jnp.bfloat16)
                for f in range(frames):
                    gat[c, h, me, (2 * f + r) * span : (2 * f + r + 1) * span] = done[
                        f * span : (f + 1) * span
                    ]
            shared(c, h, 1).start()
            shared(c, h, 0).start()

    def gathered_in(c):
        for h in range(CHUNK_HEADS):
            shared_in(c, h, 0).wait_recv()
            shared_in(c, h, 2).wait_recv()
        for s in range(n_t):
            weights_in(c, s).wait()

    def project(c, cols):
        lhs = jnp.concatenate([gat[c, h, s] for s in range(n_t) for h in range(CHUNK_HEADS)], axis=1)
        return acc[:, cols] + jnp.dot(lhs, wbuf[c, :, cols], preferred_element_type=jnp.float32)

    consts[0].wait()
    consts[1].wait()
    halo_start(0)

    @pl.loop(0, chunks + 1)
    def _(s):
        @pl.when(s + 1 < chunks)
        def _():
            halo_start(s + 1)

        @pl.when(s >= 2)
        def _():
            gathered_in(s - 2)

            @pl.loop(0, acc.shape[1] // OUT_TILE)
            def _(j):
                cols = pl.ds(pl.multiple_of(j * OUT_TILE, OUT_TILE), OUT_TILE)
                acc[:, cols] = project(s - 2, cols)

        @pl.when(s >= 1)
        def _():
            for h in range(CHUNK_HEADS):
                shared_in(s - 1, h, 1).wait_recv()
                shared(s - 1, h, 2).start()

        @pl.when(s < chunks)
        def _():
            attend(s)

    consts[2].wait()
    gathered_in(chunks - 1)
    written = []
    for j in range(acc.shape[1] // OUT_TILE):
        cols = slice(j * OUT_TILE, (j + 1) * OUT_TILE)
        gate = gate_ref[cols].reshape(1, OUT_TILE)
        total = project(chunks - 1, cols)
        out[:, cols] = (res[:, cols].astype(jnp.float32) + gate * total).astype(out.dtype)
        copy = pltpu.make_async_copy(out.at[:, cols], out_hbm.at[:, cols], o_sem.at[j])
        copy.start()
        written.append(copy)

    @pl.loop(0, chunks)
    def _(c):
        for a in range(3):
            for d in range(1, n_t):
                sent(a, c, d, me).wait_send()
        for a in range(2):

            @pl.when(has_up)
            def _():
                for f in range(frames):
                    edge(0, a, c, f).wait_send()

            @pl.when(has_down)
            def _():
                for f in range(frames):
                    edge(1, a, c, f).wait_send()

        for kind in range(3):
            for h in range(CHUNK_HEADS):
                shared(c, h, kind).wait_send()

    for copy in written:
        copy.wait()


def shards(residual, queries, key_rows, value_rows, w_out, out_gate, extents):
    n_t, n_s = lax.axis_size("tensor"), lax.axis_size("seq")
    rows, inner = queries.shape
    tokens, out_cols = residual.shape
    inner_dev = inner // n_t
    width = CHUNK_HEADS * HEAD_DIM
    if n_t != 4 or n_s < 2 or rows % 16 or inner_dev % width or out_cols % OUT_TILE:
        return plain_shards(
            residual, queries, key_rows, value_rows, w_out, out_gate, extents
        )
    chunks = inner_dev // width
    frames = tokens // (HT_DEV * WT * TILE)
    half = tokens // HT_DEV
    q_feat, k_feat = mask_features(frames)
    hbm = pl.BlockSpec(memory_space=pl.ANY)
    vmem = pl.BlockSpec(memory_space=pltpu.VMEM)
    dma = pltpu.SemaphoreType.DMA
    bf16 = jnp.bfloat16
    return pl.pallas_call(
        functools.partial(kernel, n_t, n_s, frames),
        out_shape=jax.ShapeDtypeStruct((tokens, out_cols), bf16),
        in_specs=[hbm] * 7 + [vmem, pl.BlockSpec(memory_space=pltpu.SMEM)],
        out_specs=hbm,
        scratch_shapes=[
            pltpu.VMEM((3, chunks, tokens, width), bf16),
            pltpu.VMEM((2, 2, chunks, half, width), bf16),
            pltpu.VMEM((chunks, CHUNK_HEADS, n_t, tokens, HEAD_DIM), bf16),
            pltpu.VMEM((chunks, n_t * width, out_cols), bf16),
            pltpu.VMEM((tokens, out_cols), bf16),
            pltpu.VMEM((tokens, out_cols), jnp.float32),
            pltpu.VMEM((tokens, out_cols), bf16),
            pltpu.VMEM(q_feat.shape, bf16),
            pltpu.VMEM(k_feat.shape, bf16),
            dma((3, chunks, n_t - 1)),
            dma((3, chunks, n_t - 1)),
            dma((3, chunks)),
            dma((2, 2, chunks, frames)),
            dma((2, 2, chunks, frames)),
            dma((chunks, CHUNK_HEADS, 3)),
            dma((chunks, CHUNK_HEADS, 3)),
            dma((chunks, n_t)),
            dma((3,)),
            dma((out_cols // OUT_TILE,)),
        ],
        compiler_params=pltpu.CompilerParams(
            collective_id=0, has_side_effects=True, vmem_limit_bytes=56 << 20
        ),
    )(
        queries, key_rows, value_rows, w_out, residual, q_feat, k_feat, out_gate, extents.T,
    )


def solution(mesh):
    placed = (
        P("seq", "tensor"),
        P(("seq", "tensor"), None),
        P(("seq", "tensor"), None),
        P(("seq", "tensor"), None),
        P(None, "tensor"),
        P("tensor"),
        P(),
    )
    return jax.shard_map(
        shards, mesh=mesh, in_specs=placed, out_specs=P("seq", "tensor"), check_vma=False
    )
```

```python
import functools
import math

import jax
import jax.numpy as jnp
import numpy as np
from jax import lax
from jax.experimental import pallas as pl
from jax.experimental.pallas import tpu as pltpu
from jax.sharding import PartitionSpec as P

HEAD_DIM = 128
TILE = 32
HT_DEV = 2
WT = 3
CHUNK_HEADS = 2
OUT_TILE = 512
FAR = -1e30
MESH = pl.DeviceIdType.MESH


def passed_along(value, axis, by):
    length = lax.axis_size(axis)
    pairs = [(i, i + by) for i in range(length) if 0 <= i + by < length]
    return lax.ppermute(value, axis, pairs)


def tile_coords(row_count, tile_rows, first_row):
    position = jnp.arange(row_count, dtype=jnp.int32)
    frame_id = position // (tile_rows * WT * TILE)
    row_id = first_row + position // (WT * TILE) % tile_rows
    col_id = position // TILE % WT
    return (frame_id, row_id, col_id)


def allowed_keys(query_place, key_place, head_reach, seq_block, seq_count):
    frame_gap = jnp.abs(query_place[0][:, None] - key_place[0][None, :])
    row_gap = jnp.abs(query_place[1][:, None] - key_place[1][None, :])
    col_gap = jnp.abs(query_place[2][:, None] - key_place[2][None, :])
    global_row = key_place[1] + seq_block * HT_DEV
    inside = (global_row >= 0) & (global_row < seq_count * HT_DEV)
    return (
        (frame_gap[None] <= head_reach[:, 0, None, None])
        & (row_gap[None] <= head_reach[:, 1, None, None])
        & (col_gap[None] <= head_reach[:, 2, None, None])
        & inside[None, None, :]
    )


def plain_shards(residual, queries, key_rows, value_rows, w_out, out_gate, extents):
    head_q, head_k, head_v = (
        lax.all_to_all(queries, "tensor", split_axis=1, concat_axis=0, tiled=True),
        lax.all_to_all(key_rows, "tensor", split_axis=1, concat_axis=0, tiled=True),
        lax.all_to_all(value_rows, "tensor", split_axis=1, concat_axis=0, tiled=True),
    )
    tokens, inner_dev = head_q.shape
    heads_here = inner_dev // HEAD_DIM
    seq_block = lax.axis_index("seq")
    seq_count = lax.axis_size("seq")
    head_reach = lax.dynamic_slice_in_dim(
        extents, lax.axis_index("tensor") * heads_here, heads_here, 0
    )
    query_tiles = head_q.reshape(tokens, heads_here, HEAD_DIM)
    query_place = tile_coords(tokens, HT_DEV, 0)
    stacked = jnp.stack([head_k, head_v])

    def part_scores(pair_rows, key_place):
        key_tiles = pair_rows[0].reshape(-1, heads_here, HEAD_DIM)
        scores = jnp.einsum(
            "qhd,khd->hqk", query_tiles, key_tiles, preferred_element_type=jnp.float32
        ) / math.sqrt(HEAD_DIM)
        allowed = allowed_keys(query_place, key_place, head_reach, seq_block, seq_count)
        return jnp.where(allowed, scores, FAR)

    by_row = stacked.reshape(2, -1, HT_DEV, WT * TILE, inner_dev)
    halves = tokens // HT_DEV
    last_row = by_row[:, :, HT_DEV - 1].reshape(2, halves, inner_dev)
    first_row = by_row[:, :, 0].reshape(2, halves, inner_dev)
    parts = [
        (stacked, query_place),
        (passed_along(last_row, "seq", 1), tile_coords(halves, 1, -1)),
        (passed_along(first_row, "seq", -1), tile_coords(halves, 1, HT_DEV)),
    ]
    scores = jnp.concatenate([part_scores(*part) for part in parts], axis=-1)
    value_all = jnp.concatenate([pair_rows[1] for pair_rows, _ in parts], axis=0)
    row_max = jnp.max(scores, axis=-1, keepdims=True)
    exp_scores = jnp.exp(scores - row_max)
    row_sum = jnp.sum(exp_scores, axis=-1, keepdims=True)
    weights = (exp_scores / row_sum).astype(jnp.bfloat16)
    attended = jnp.einsum(
        "hqk,khd->qhd",
        weights,
        value_all.reshape(-1, heads_here, HEAD_DIM),
        preferred_element_type=jnp.float32,
    )
    head_out = attended.reshape(tokens, inner_dev).astype(jnp.bfloat16)
    projected = jnp.dot(
        lax.all_gather(head_out, "tensor", axis=1, tiled=True),
        w_out,
        preferred_element_type=jnp.float32,
    )
    return (residual.astype(jnp.float32) + out_gate * projected).astype(jnp.bfloat16)


def mask_features(frames):
    span = WT * TILE
    q_feat = np.zeros((2, frames * span, HEAD_DIM), np.float32)
    k_feat = np.zeros((2, frames * 3 * span, HEAD_DIM), np.float32)
    q_at = np.arange(frames * span)
    q_frame, q_col = q_at // span, q_at // TILE % WT
    k_at = np.arange(frames * 3 * span)
    k_frame, k_col = k_at // (3 * span), k_at // TILE % WT
    k_row = k_at // span % 3 - 1
    for r in range(2):
        for j in range(3):
            q_feat[r, :, j] = q_feat[r, :, 8 + j] = q_frame == j
            q_feat[r, :, 3 + j] = q_feat[r, :, 11 + j] = q_col == j
            k_feat[r, :, j] = FAR * (abs(k_frame - j) >= 2)
            k_feat[r, :, 8 + j] = FAR * (abs(k_frame - j) == 1)
            k_feat[r, :, 3 + j] = FAR * (abs(k_col - j) >= 2)
            k_feat[r, :, 11 + j] = FAR * (abs(k_col - j) == 1)
        q_feat[r, :, 14:17] = 1.0
        k_feat[r, :, 14] = FAR * (k_row != 0)
    k_feat[0, :, 15] = FAR * (k_row == -1)
    k_feat[1, :, 16] = FAR * (k_row == 1)
    return jnp.asarray(q_feat, jnp.bfloat16), jnp.asarray(k_feat, jnp.bfloat16)


def kernel(
    n_t, n_s, frames, q_hbm, k_hbm, v_hbm, w_hbm, res_hbm, qf_hbm, kf_hbm, gate_ref, ext_ref,
    out_hbm, own, halo, gat, wbuf, res, acc, out, qf, kf,
    a_send, a_recv, a_loc, h_send, h_recv, g_send, g_recv, w_sem, c_sem, o_sem,
):
    rows = q_hbm.shape[0]
    inner_dev = q_hbm.shape[1] // n_t
    width = CHUNK_HEADS * HEAD_DIM
    chunks = inner_dev // width
    span = WT * TILE
    me, sb = lax.axis_index("tensor"), lax.axis_index("seq")
    mate = me // 2 * 2 + 1 - lax.rem(me, 2)
    across = lax.rem(me + n_t // 2, n_t)
    srcs = (k_hbm, v_hbm, q_hbm)
    has_up, has_down = sb < n_s - 1, sb > 0

    barrier = pltpu.get_barrier_semaphore()
    for d in range(1, n_t):
        pl.semaphore_signal(
            barrier, inc=1, device_id={"tensor": lax.rem(me + d, n_t)}, device_id_type=MESH
        )

    @pl.when(has_up)
    def _():
        pl.semaphore_signal(barrier, inc=1, device_id={"seq": sb + 1}, device_id_type=MESH)

    @pl.when(has_down)
    def _():
        pl.semaphore_signal(barrier, inc=1, device_id={"seq": sb - 1}, device_id_type=MESH)

    inner_block = has_up & has_down

    @pl.when(inner_block)
    def _():
        pl.semaphore_wait(barrier, n_t + 1)

    @pl.when(jnp.logical_not(inner_block))
    def _():
        pl.semaphore_wait(barrier, n_t)

    def columns(owner, c):
        return pl.ds(pl.multiple_of(owner * inner_dev + c * width, width), width)

    def slot(owner):
        return pl.ds(pl.multiple_of(owner * rows, 16), rows)

    def sent(a, c, d, owner):
        peer = lax.rem(me + d, n_t)
        return pltpu.make_async_remote_copy(
            src_ref=srcs[a].at[:, columns(peer, c)],
            dst_ref=own.at[a, c, slot(owner), :],
            send_sem=a_send.at[a, c, d - 1],
            recv_sem=a_recv.at[a, c, d - 1],
            device_id={"tensor": peer},
            device_id_type=MESH,
        )

    def kept(a, c):
        return pltpu.make_async_copy(
            srcs[a].at[:, columns(me, c)], own.at[a, c, slot(me), :], a_loc.at[a, c]
        )

    def arrived(a, c):
        for d in range(1, n_t):
            sent(a, c, d, lax.rem(me - d + n_t, n_t)).wait_recv()
        kept(a, c).wait()

    def edge(way, a, c, f):
        first = f * 2 * span + (span if way == 0 else 0)
        return pltpu.make_async_remote_copy(
            src_ref=own.at[a, c, pl.ds(first, span), :],
            dst_ref=halo.at[way, a, c, pl.ds(f * span, span), :],
            send_sem=h_send.at[way, a, c, f],
            recv_sem=h_recv.at[way, a, c, f],
            device_id={"seq": sb + 1 if way == 0 else sb - 1},
            device_id_type=MESH,
        )

    def shared(c, h, kind):
        piece = across if kind == 2 else me
        return pltpu.make_async_remote_copy(
            src_ref=gat.at[c, h, piece],
            dst_ref=gat.at[c, h, piece],
            send_sem=g_send.at[c, h, kind],
            recv_sem=g_recv.at[c, h, kind],
            device_id={"tensor": across if kind == 1 else mate},
            device_id_type=MESH,
        )

    def shared_in(c, h, kind):
        piece = (mate, across, lax.rem(mate + n_t // 2, n_t))[kind]
        return pltpu.make_async_remote_copy(
            src_ref=gat.at[c, h, piece],
            dst_ref=gat.at[c, h, piece],
            send_sem=g_send.at[c, h, kind],
            recv_sem=g_recv.at[c, h, kind],
            device_id={"tensor": across if kind == 1 else mate},
            device_id_type=MESH,
        )

    def weights_in(c, s):
        return pltpu.make_async_copy(
            w_hbm.at[pl.ds(pl.multiple_of(s * inner_dev + c * width, width), width), :],
            wbuf.at[c, pl.ds(s * width, width), :],
            w_sem.at[c, s],
        )

    @pl.loop(0, chunks)
    def _(c):
        for a in range(3):
            for d in (2, 1, 3):
                sent(a, c, d, me).start()
            kept(a, c).start()

    @pl.loop(0, chunks)
    def _(c):
        for s in range(n_t):
            weights_in(c, s).start()

    consts = [
        pltpu.make_async_copy(src, dst, c_sem.at[i])
        for i, (src, dst) in enumerate(((qf_hbm, qf), (kf_hbm, kf), (res_hbm, res)))
    ]
    for copy in consts:
        copy.start()
    acc[...] = jnp.zeros_like(acc)

    @pl.when(sb == 0)
    def _():
        halo[0] = jnp.zeros(halo.shape[1:], halo.dtype)

    @pl.when(sb == n_s - 1)
    def _():
        halo[1] = jnp.zeros(halo.shape[1:], halo.dtype)

    def halo_start(c):
        for a in range(2):
            arrived(a, c)

            @pl.when(has_up)
            def _():
                for f in range(frames):
                    edge(0, a, c, f).start()

            @pl.when(has_down)
            def _():
                for f in range(frames):
                    edge(1, a, c, f).start()

    def gathered(a, c, r, lanes):
        parts = []
        for f in range(frames):
            near = own[a, c, f * 2 * span : (f + 1) * 2 * span, lanes]
            far = halo[r, a, c, f * span : (f + 1) * span, lanes]
            parts += [far, near] if r == 0 else [near, far]
        return jnp.concatenate(parts, axis=0)

    def switches(head):
        lane = lax.broadcasted_iota(jnp.int32, (1, HEAD_DIM), 1)
        at = me * (inner_dev // HEAD_DIM) + head
        coef = jnp.where(lane < 8, 1.0, 0.0)
        for d, first, last in ((0, 8, 11), (2, 11, 14), (1, 14, 15)):
            stop = (1 - ext_ref[d, at]).astype(jnp.float32)
            coef = jnp.where((lane >= first) & (lane < last), stop, coef)
        coef = jnp.where(lane == 15, jnp.where(sb == 0, 1.0, 0.0), coef)
        return jnp.where(lane == 16, jnp.where(sb == n_s - 1, 1.0, 0.0), coef)

    def attend(c):
        arrived(2, c)
        for a in range(2):

            @pl.when(has_down)
            def _():
                for f in range(frames):
                    edge(0, a, c, f).wait_recv()

            @pl.when(has_up)
            def _():
                for f in range(frames):
                    edge(1, a, c, f).wait_recv()

        ones = jnp.ones((frames * 3 * span, HEAD_DIM), jnp.bfloat16)
        for h in range(CHUNK_HEADS):
            lanes = slice(h * HEAD_DIM, (h + 1) * HEAD_DIM)
            coef = switches(c * CHUNK_HEADS + h)
            for r in range(2):
                q_part = jnp.concatenate(
                    [own[2, c, (2 * f + r) * span : (2 * f + r + 1) * span, lanes]
                     for f in range(frames)], axis=0)
                q_feat = (qf[r].astype(jnp.float32) * coef).astype(jnp.bfloat16)
                scores = lax.dot_general(
                    jnp.concatenate([q_part, q_feat], axis=1),
                    jnp.concatenate([gathered(0, c, r, lanes), kf[r]], axis=1),
                    (((1,), (1,)), ((), ())),
                    preferred_element_type=jnp.float32,
                )
                top = jnp.max(scores, axis=-1, keepdims=True)
                weights = jnp.exp2(
                    (scores - top) * (math.log2(math.e) / math.sqrt(HEAD_DIM))
                ).astype(jnp.bfloat16)
                both = jnp.dot(
                    weights,
                    jnp.concatenate([gathered(1, c, r, lanes), ones], axis=1),
                    preferred_element_type=jnp.float32,
                )
                done = (both[:, :HEAD_DIM] / both[:, HEAD_DIM:]).astype(jnp.bfloat16)
                for f in range(frames):
                    gat[c, h, me, (2 * f + r) * span : (2 * f + r + 1) * span] = done[
                        f * span : (f + 1) * span
                    ]
            shared(c, h, 1).start()
            shared(c, h, 0).start()

    def gathered_in(c):
        for h in range(CHUNK_HEADS):
            shared_in(c, h, 0).wait_recv()
            shared_in(c, h, 2).wait_recv()
        for s in range(n_t):
            weights_in(c, s).wait()

    def project(c, cols):
        lhs = jnp.concatenate([gat[c, h, s] for s in range(n_t) for h in range(CHUNK_HEADS)], axis=1)
        return acc[:, cols] + jnp.dot(lhs, wbuf[c, :, cols], preferred_element_type=jnp.float32)

    consts[0].wait()
    consts[1].wait()
    halo_start(0)

    def forward(c):
        for h in range(CHUNK_HEADS):
            shared_in(c, h, 1).wait_recv()
            shared(c, h, 2).start()

    def accumulate(c):
        gathered_in(c)

        @pl.loop(0, acc.shape[1] // OUT_TILE)
        def _(j):
            cols = pl.ds(pl.multiple_of(j * OUT_TILE, OUT_TILE), OUT_TILE)
            acc[:, cols] = project(c, cols)

    early = chunks - 2

    @pl.loop(0, chunks)
    def _(s):
        @pl.when(s + 1 < chunks)
        def _():
            halo_start(s + 1)

        @pl.when(s == chunks - 1)
        def _():
            @pl.loop(0, early)
            def _(c):
                @pl.when(c >= 1)
                def _():
                    accumulate(c - 1)

                forward(c)

        attend(s)

    @pl.loop(early, chunks)
    def _(c):
        @pl.when(c >= 1)
        def _():
            accumulate(c - 1)

        forward(c)

    consts[2].wait()
    gathered_in(chunks - 1)
    written = []
    for j in range(acc.shape[1] // OUT_TILE):
        cols = slice(j * OUT_TILE, (j + 1) * OUT_TILE)
        gate = gate_ref[cols].reshape(1, OUT_TILE)
        total = project(chunks - 1, cols)
        out[:, cols] = (res[:, cols].astype(jnp.float32) + gate * total).astype(out.dtype)
        copy = pltpu.make_async_copy(out.at[:, cols], out_hbm.at[:, cols], o_sem.at[j])
        copy.start()
        written.append(copy)

    @pl.loop(0, chunks)
    def _(c):
        for a in range(3):
            for d in range(1, n_t):
                sent(a, c, d, me).wait_send()
        for a in range(2):

            @pl.when(has_up)
            def _():
                for f in range(frames):
                    edge(0, a, c, f).wait_send()

            @pl.when(has_down)
            def _():
                for f in range(frames):
                    edge(1, a, c, f).wait_send()

        for kind in range(3):
            for h in range(CHUNK_HEADS):
                shared(c, h, kind).wait_send()

    for copy in written:
        copy.wait()


def shards(residual, queries, key_rows, value_rows, w_out, out_gate, extents):
    n_t, n_s = lax.axis_size("tensor"), lax.axis_size("seq")
    rows, inner = queries.shape
    tokens, out_cols = residual.shape
    inner_dev = inner // n_t
    width = CHUNK_HEADS * HEAD_DIM
    if n_t != 4 or n_s < 2 or rows % 16 or inner_dev % width or out_cols % OUT_TILE:
        return plain_shards(
            residual, queries, key_rows, value_rows, w_out, out_gate, extents
        )
    chunks = inner_dev // width
    frames = tokens // (HT_DEV * WT * TILE)
    half = tokens // HT_DEV
    q_feat, k_feat = mask_features(frames)
    hbm = pl.BlockSpec(memory_space=pl.ANY)
    vmem = pl.BlockSpec(memory_space=pltpu.VMEM)
    dma = pltpu.SemaphoreType.DMA
    bf16 = jnp.bfloat16
    return pl.pallas_call(
        functools.partial(kernel, n_t, n_s, frames),
        out_shape=jax.ShapeDtypeStruct((tokens, out_cols), bf16),
        in_specs=[hbm] * 7 + [vmem, pl.BlockSpec(memory_space=pltpu.SMEM)],
        out_specs=hbm,
        scratch_shapes=[
            pltpu.VMEM((3, chunks, tokens, width), bf16),
            pltpu.VMEM((2, 2, chunks, half, width), bf16),
            pltpu.VMEM((chunks, CHUNK_HEADS, n_t, tokens, HEAD_DIM), bf16),
            pltpu.VMEM((chunks, n_t * width, out_cols), bf16),
            pltpu.VMEM((tokens, out_cols), bf16),
            pltpu.VMEM((tokens, out_cols), jnp.float32),
            pltpu.VMEM((tokens, out_cols), bf16),
            pltpu.VMEM(q_feat.shape, bf16),
            pltpu.VMEM(k_feat.shape, bf16),
            dma((3, chunks, n_t - 1)),
            dma((3, chunks, n_t - 1)),
            dma((3, chunks)),
            dma((2, 2, chunks, frames)),
            dma((2, 2, chunks, frames)),
            dma((chunks, CHUNK_HEADS, 3)),
            dma((chunks, CHUNK_HEADS, 3)),
            dma((chunks, n_t)),
            dma((3,)),
            dma((out_cols // OUT_TILE,)),
        ],
        compiler_params=pltpu.CompilerParams(
            collective_id=0, has_side_effects=True, vmem_limit_bytes=56 << 20
        ),
    )(
        queries, key_rows, value_rows, w_out, residual, q_feat, k_feat, out_gate, extents.T,
    )


def solution(mesh):
    placed = (
        P("seq", "tensor"),
        P(("seq", "tensor"), None),
        P(("seq", "tensor"), None),
        P(("seq", "tensor"), None),
        P(None, "tensor"),
        P("tensor"),
        P(),
    )
    return jax.shard_map(
        shards, mesh=mesh, in_specs=placed, out_specs=P("seq", "tensor"), check_vma=False
    )
```
